256 devices in a mesh: seg: 16 (over x, y_hi, core), gx: 16 (over z, y_lo).
Axes of the slice: x: 4, y: 4 (y_hi: 2, y_lo: 2; y = y_hi * 2 + y_lo), z: 8, core: 2. Of those that a mesh axis runs over, the one named last changes fastest.
Arguments:
- adjoint_in: float32 [16, 5, 256, 32, 512], P('seg', None, 'gx'), may hold values from -6 to 6
- sensor: float32 [16, 256, 32, 512], P('seg', 'gx'), may hold values from 0.06 to 0.15
- filter_matrix: float32 [512, 512], replicated
- coupling: float32 [5, 5], replicated
Outputs:
- adjoint_out: float32 [16, 5, 256, 32, 512], P('seg', None, 'gx')
The draws below stay inside these ranges and needn't reach their ends.
All inputs are finite; a program needn't handle non-finite values.
Results may differ from the reference program's by a relative error of at most 0.00017.
Values sent between devices are 32-bit elements; how exact they have to be, the bound alone decides.
A program may use at most 64 MiB of HBM per device.

```python
import math
import jax
import jax.numpy as jnp
from jax import lax

FIELDS = 5
NR = 512
STEPS = 3
CX = 16
NTH = 32
NSEG = 16
NX = 256


def draw_adjoint_in(key, part):
    level_key = jax.random.fold_in(key, 11)
    noise_key = jax.random.fold_in(key, 23)
    blocks = NX // CX
    levels = jnp.exp(jax.random.uniform(level_key, (NSEG, 1, blocks, 1, 1, 1), jnp.float32, -3.0, 1.0))
    shape = (NSEG, FIELDS, blocks, CX, NTH, NR)
    noise = jax.random.truncated_normal(noise_key, -4.0, 4.0, shape, jnp.float32)
    values = jnp.clip(noise * levels, -6.0, 6.0)
    return values.reshape(NSEG, FIELDS, NX, NTH, NR)


def draw_filter_matrix(key, part):
    noise = jax.random.truncated_normal(key, -4.0, 4.0, (NR, NR), jnp.float32)
    return 0.6 * jnp.eye(NR, dtype=jnp.float32) + noise * (0.5 / math.sqrt(NR))


def draw_coupling(key, part):
    noise = jax.random.truncated_normal(key, -4.0, 4.0, (FIELDS, FIELDS), jnp.float32)
    return jnp.eye(FIELDS, dtype=jnp.float32) + 0.25 * noise


def shard_levels(own_key, shape, cuts, smallest, high):
    def one(dim, parts):
        draws = jax.random.uniform(jax.random.fold_in(jax.random.fold_in(own_key, 6), dim), (parts,), jnp.float32, smallest / len(cuts), high / len(cuts))
        return jnp.repeat(jnp.exp(draws), shape[dim] // parts).reshape((-1,) + (1,) * (len(shape) - dim - 1))

    level = one(*cuts[0])
    for cut in cuts[1:]:
        level = level * one(*cut)
    return level


def setup_inputs(seed: int = 0) -> dict:
    key_of = jax.random.split(jax.random.key(seed), 5)
    adjoint_in = draw_adjoint_in(jax.random.fold_in(key_of[4], 71), 0)
    sensor = jnp.clip(jnp.exp(math.log(0.15) - 0.9162908 * jax.random.uniform(key_of[1], (NSEG, NX, NTH, NR), jnp.float32) ** shard_levels(key_of[1], (NSEG, NX, NTH, NR), ((0, 16), (1, 16)), -0.2, 0.2)), 0.06, 0.15)
    filter_matrix = draw_filter_matrix(jax.random.fold_in(key_of[4], 71), 0)
    coupling = draw_coupling(jax.random.fold_in(key_of[4], 71), 0)
    return dict(adjoint_in=adjoint_in, sensor=sensor, filter_matrix=filter_matrix, coupling=coupling)


def filter_rows(state, filter_matrix):
    dims_shape = state.shape
    flat = state.reshape(-1, dims_shape[-1])
    result = jnp.dot(flat, filter_matrix, precision=lax.Precision.HIGHEST, preferred_element_type=jnp.float32)
    return result.reshape(dims_shape)


def mix_fields(filtered, coupling):
    return jnp.einsum("gf,gxyr->fxyr", coupling, filtered, precision=lax.Precision.HIGHEST)


def laplace(padded):
    middle = padded[:, 1:-1]
    widened = jnp.pad(middle, ((0, 0), (0, 0), (1, 1), (1, 1)))
    laplacian = padded[:, 2:] + padded[:, :-2]
    laplacian = laplacian + widened[:, :, 2:, 1:-1] + widened[:, :, :-2, 1:-1]
    laplacian = laplacian + widened[:, :, 1:-1, 2:] + widened[:, :, 1:-1, :-2]
    return laplacian - 6.0 * middle


def reference(adjoint_in, sensor, filter_matrix, coupling):
    incoming = jnp.roll(adjoint_in, -1, axis=0)

    def propagate(inputs_pair):
        state, sensor_cell = inputs_pair
        for step in range(STEPS):
            filtered = filter_rows(state, filter_matrix)
            mixed = mix_fields(filtered, coupling)
            padded = jnp.pad(mixed, ((0, 0), (1, 1), (0, 0), (0, 0)))
            state = filtered + sensor_cell[None] * laplace(padded)
        return state

    carried = lax.map(propagate, (incoming, sensor))
    return carried - adjoint_in
```

```python
import functools

import jax
import jax.numpy as jnp
from jax import lax
from jax.experimental import pallas as pl
from jax.experimental.pallas import tpu as pltpu
from jax.sharding import PartitionSpec as P

STEPS = 3
FIRST = 2
MESH = pl.DeviceIdType.MESH


def kernel(a_ref, s_ref, w_ref, c_ref, out_ref, planes, own, sens, wide, wcat, xcat, filt, mixd, ssem, rsem, lsem, gsem):
    fields, cx, nt, nr = out_ref.shape
    total = cx + 2 * STEPS
    half = nt // 2
    seg, gx = lax.axis_index("seg"), lax.axis_index("gx")
    nseg, ngx = lax.axis_size("seg"), lax.axis_size("gx")
    after, before = lax.rem(seg + 1, nseg), lax.rem(seg + nseg - 1, nseg)
    has_low, has_high = gx > 0, gx < ngx - 1
    low, high = jnp.maximum(gx - 1, 0), jnp.minimum(gx + 1, ngx - 1)
    lows, highs = has_low.astype(jnp.int32), has_high.astype(jnp.int32)
    leaves = lax.rem(seg, 2) == 0
    crosses = jnp.logical_and(leaves, lax.rem(lax.div(seg, 2), 2) == 0)
    held = jnp.where(crosses, lax.rem(seg + nseg - 4, nseg), seg)
    freed = jnp.where(crosses, lax.rem(seg + 4, nseg), seg)

    barrier = pltpu.get_barrier_semaphore()

    def greet(device):
        pl.semaphore_signal(barrier, inc=1, device_id=device, device_id_type=MESH)

    greet((after, gx))

    @pl.when(has_low)
    def _():
        greet((after, low))
        greet((seg, low))

    @pl.when(has_high)
    def _():
        greet((after, high))
        greet((seg, high))

    @pl.when(jnp.logical_and(crosses, has_low))
    def _():
        greet((held, low))

    @pl.when(jnp.logical_and(crosses, has_high))
    def _():
        greet((held, high))

    def own_copy(i):
        return pltpu.make_async_copy(a_ref.at[0, :, i], own.at[i], lsem.at[2 + i])

    w_copy = pltpu.make_async_copy(w_ref, wide, lsem.at[0])
    s_copy = pltpu.make_async_copy(s_ref.at[0], sens.at[pl.ds(2, cx)], lsem.at[1])
    w_copy.start()
    s_copy.start()
    for j in range(cx):
        own_copy(j).start()

    def plane_copy(source, slot, sem, device):
        return pltpu.make_async_remote_copy(
            src_ref=a_ref.at[0, :, source],
            dst_ref=planes.at[slot],
            send_sem=ssem.at[sem],
            recv_sem=rsem.at[slot],
            device_id=device,
            device_id_type=MESH,
        )

    def sens_copy(source, slot, sem, device):
        return pltpu.make_async_remote_copy(
            src_ref=s_ref.at[0, pl.ds(source, 2)],
            dst_ref=sens.at[pl.ds(slot, 2)],
            send_sem=ssem.at[total + sem],
            recv_sem=rsem.at[total + sem],
            device_id=device,
            device_id_type=MESH,
        )

    def to_high(j):
        return plane_copy(cx - STEPS + j, j, j, (before, high))

    def to_same(j):
        return plane_copy(j, STEPS + j, STEPS + j, (before, gx))

    def to_low(j):
        return plane_copy(j, STEPS + cx + j, STEPS + cx + j, (before, low))

    sens_to_high = sens_copy(cx - 2, 0, 0, (seg, high))
    sens_to_low = sens_copy(0, cx + 2, 1, (seg, low))

    pl.semaphore_wait(barrier, 1 + (2 + crosses.astype(jnp.int32)) * (lows + highs))

    @pl.when(has_high)
    def _():
        sens_to_high.start()

    @pl.when(has_low)
    def _():
        sens_to_low.start()

    for j in range(STEPS):

        @pl.when(has_high)
        def _():
            to_high(j).start()

        @pl.when(has_low)
        def _():
            to_low(j).start()

    for j in range(FIRST):
        to_same(j).start()

    @pl.when(jnp.logical_not(leaves))
    def _():
        for j in range(FIRST, cx):
            to_same(j).start()

    @pl.when(jnp.logical_not(has_low))
    def _():
        sens[pl.ds(0, 2)] = jnp.zeros((2, nt, nr), jnp.float32)
        planes[pl.ds(0, STEPS)] = jnp.zeros((STEPS, fields, nt, nr), jnp.float32)

    @pl.when(jnp.logical_not(has_high))
    def _():
        sens[pl.ds(cx + 2, 2)] = jnp.zeros((2, nt, nr), jnp.float32)
        planes[pl.ds(cx + STEPS, STEPS)] = jnp.zeros((STEPS, fields, nt, nr), jnp.float32)

    for step in range(STEPS):
        for slot in range(3):
            for f in range(fields):
                mixd[step, slot, f, pl.ds(0, 8)] = jnp.zeros((8, nr), jnp.float32)
                mixd[step, slot, f, pl.ds(8 + nt, 8)] = jnp.zeros((8, nr), jnp.float32)

    w_copy.wait()
    block = 64
    for i in range(nr // block):
        w = wide[pl.ds(i * block, block)]
        w_hi = w.astype(jnp.bfloat16)
        w_lo = (w - w_hi.astype(jnp.float32)).astype(jnp.bfloat16)
        wcat[pl.ds(i * block, block)] = w_hi
        wcat[pl.ds(nr + i * block, block)] = w_hi
        wcat[pl.ds(2 * nr + i * block, block)] = w_lo
    s_copy.wait()

    @pl.when(has_low)
    def _():
        sens_copy(cx - 2, 0, 0, (seg, high)).wait_recv()

    @pl.when(has_high)
    def _():
        sens_copy(0, cx + 2, 1, (seg, low)).wait_recv()

    def arrival(i):
        plane_copy(0, i, i, (before, gx)).wait_recv()

    @pl.when(jnp.logical_and(leaves, has_low))
    def _():
        for j in range(STEPS):
            arrival(j)
        pl.semaphore_signal(gsem, inc=1, device_id=(freed, low), device_id_type=MESH)

    @pl.when(jnp.logical_and(leaves, has_high))
    def _():
        for j in range(STEPS):
            arrival(STEPS + cx + j)
        pl.semaphore_signal(gsem, inc=1, device_id=(freed, high), device_id_type=MESH)

    @pl.when(leaves)
    def _():
        pl.semaphore_wait(gsem, lows + highs)
        for j in range(FIRST, cx):
            to_same(j).start()

    lane = lax.broadcasted_iota(jnp.int32, (half, nr), 1)

    def put(f, h, x):
        rows = pl.ds(f * nt + h * half, half)
        x_hi = x.astype(jnp.bfloat16)
        x_lo = (x - x_hi.astype(jnp.float32)).astype(jnp.bfloat16)
        xcat[rows, pl.ds(0, nr)] = x_hi
        xcat[rows, pl.ds(nr, nr)] = x_lo
        xcat[rows, pl.ds(2 * nr, nr)] = x_hi

    def filter_and_mix(step, i):
        two, three = lax.rem(i, 2), lax.rem(i, 3)
        filt[step, two] = jnp.dot(xcat[...], wcat[...], preferred_element_type=jnp.float32).reshape(fields, nt, nr)
        for t in range(nt // 8):
            rows = pl.ds(t * 8, 8)
            v = [filt[step, two, g, rows] for g in range(fields)]
            for f in range(fields):
                m = c_ref[0, f] * v[0]
                for g in range(1, fields):
                    m = m + c_ref[g, f] * v[g]
                mixd[step, three, f, pl.ds(8 + t * 8, 8)] = m

    def stencil(step, i, use):
        two = lax.rem(i, 2)
        mid, lo, hi = lax.rem(i, 3), lax.rem(i + 2, 3), lax.rem(i + 1, 3)
        for h in range(2):
            s = sens[i - 1, pl.ds(h * half, half)]
            for f in range(fields):
                at = 8 + h * half
                m = mixd[step, mid, f, pl.ds(at, half)]
                total_ = mixd[step, lo, f, pl.ds(at, half)] + mixd[step, hi, f, pl.ds(at, half)]
                total_ = total_ + mixd[step, mid, f, pl.ds(at - 1, half)] + mixd[step, mid, f, pl.ds(at + 1, half)]
                left = jnp.where(lane == 0, 0.0, pltpu.roll(m, 1, 1))
                right = jnp.where(lane == nr - 1, 0.0, pltpu.roll(m, nr - 1, 1))
                total_ = total_ + left + right - 6.0 * m
                use(f, h, filt[step, two, f, pl.ds(h * half, half)] + s * total_)

    def arrive(i, carry):
        slab = jnp.logical_and(i >= STEPS, i < STEPS + cx)
        halo = jnp.logical_or(jnp.logical_and(i < STEPS, has_low), jnp.logical_and(i >= STEPS + cx, has_high))

        @pl.when(jnp.logical_or(slab, jnp.logical_and(halo, jnp.logical_not(leaves))))
        def _():
            arrival(i)

        for h in range(2):
            for f in range(fields):
                put(f, h, planes[i, f, pl.ds(h * half, half)])
        filter_and_mix(0, i)

        @pl.when(i >= 2)
        def _():
            stencil(0, i - 1, put)
            filter_and_mix(1, i - 1)

        @pl.when(i >= 4)
        def _():
            stencil(1, i - 2, put)
            filter_and_mix(2, i - 2)

        @pl.when(i >= 6)
        def _():
            o = i - 2 * STEPS
            pltpu.make_async_copy(a_ref.at[0, :, o], own.at[o], lsem.at[2 + o]).wait()

            def write(f, h, x):
                rows = pl.ds(h * half, half)
                out_ref[f, o, rows] = x - own[o, f, rows]

            stencil(2, i - 3, write)

        return carry

    lax.fori_loop(0, total, arrive, 0)

    @pl.when(has_high)
    def _():
        sens_to_high.wait_send()
        for j in range(STEPS):
            to_high(j).wait_send()

    for j in range(cx):
        to_same(j).wait_send()

    @pl.when(has_low)
    def _():
        sens_to_low.wait_send()
        for j in range(STEPS):
            to_low(j).wait_send()


def shards(adjoint_in, sensor, filter_matrix, coupling):
    _, fields, cx, nt, nr = adjoint_in.shape
    total = cx + 2 * STEPS
    out = pl.pallas_call(
        kernel,
        out_shape=pltpu.VMEM((fields, cx, nt, nr), jnp.float32),
        in_specs=[
            pl.BlockSpec(memory_space=pltpu.HBM),
            pl.BlockSpec(memory_space=pltpu.HBM),
            pl.BlockSpec(memory_space=pltpu.HBM),
            pl.BlockSpec(memory_space=pltpu.SMEM),
        ],
        out_specs=pl.BlockSpec(memory_space=pltpu.VMEM),
        scratch_shapes=[
            pltpu.VMEM((total, fields, nt, nr), jnp.float32),
            pltpu.VMEM((cx, fields, nt, nr), jnp.float32),
            pltpu.VMEM((cx + 4, nt, nr), jnp.float32),
            pltpu.VMEM((nr, nr), jnp.float32),
            pltpu.VMEM((3 * nr, nr), jnp.bfloat16),
            pltpu.VMEM((fields * nt, 3 * nr), jnp.bfloat16),
            pltpu.VMEM((STEPS, 2, fields, nt, nr), jnp.float32),
            pltpu.VMEM((STEPS, 3, fields, nt + 16, nr), jnp.float32),
            pltpu.SemaphoreType.DMA((total + 2,)),
            pltpu.SemaphoreType.DMA((total + 2,)),
            pltpu.SemaphoreType.DMA((cx + 2,)),
            pltpu.SemaphoreType.REGULAR,
        ],
        compiler_params=pltpu.CompilerParams(collective_id=0, has_side_effects=True, vmem_limit_bytes=61_400_000),
        name="shooting",
    )(adjoint_in, sensor, filter_matrix, coupling)
    return out[None]


def solution(mesh):
    in_specs = (P("seg", None, "gx", None, None), P("seg", "gx", None, None), P(), P())
    out_specs = P("seg", None, "gx", None, None)
    return jax.shard_map(shards, mesh=mesh, in_specs=in_specs, out_specs=out_specs, check_vma=False)
```

```python
import functools

import jax
import jax.numpy as jnp
from jax import lax
from jax.experimental import pallas as pl
from jax.experimental.pallas import tpu as pltpu
from jax.sharding import PartitionSpec as P

STEPS = 3
FIRST, SECOND = 2, 2
MESH = pl.DeviceIdType.MESH


def kernel(a_ref, s_ref, w_ref, c_ref, out_ref, planes, own, sens, wide, wcat, xcat, filt, mixd, ssem, rsem, lsem, gsem):
    fields, cx, nt, nr = out_ref.shape
    total = cx + 2 * STEPS
    half = nt // 2
    seg, gx = lax.axis_index("seg"), lax.axis_index("gx")
    nseg, ngx = lax.axis_size("seg"), lax.axis_size("gx")
    after, before = lax.rem(seg + 1, nseg), lax.rem(seg + nseg - 1, nseg)
    has_low, has_high = gx > 0, gx < ngx - 1
    low, high = jnp.maximum(gx - 1, 0), jnp.minimum(gx + 1, ngx - 1)
    lows, highs = has_low.astype(jnp.int32), has_high.astype(jnp.int32)
    leaves = lax.rem(seg, 2) == 0
    crosses = jnp.logical_and(leaves, lax.rem(lax.div(seg, 2), 2) == 0)
    held = jnp.where(crosses, lax.rem(seg + nseg - 4, nseg), seg)
    freed = jnp.where(crosses, lax.rem(seg + 4, nseg), seg)

    barrier = pltpu.get_barrier_semaphore()

    def greet(device):
        pl.semaphore_signal(barrier, inc=1, device_id=device, device_id_type=MESH)

    greet((after, gx))

    @pl.when(has_low)
    def _():
        greet((after, low))
        greet((seg, low))

    @pl.when(has_high)
    def _():
        greet((after, high))
        greet((seg, high))

    @pl.when(jnp.logical_and(crosses, has_low))
    def _():
        greet((held, low))

    @pl.when(jnp.logical_and(crosses, has_high))
    def _():
        greet((held, high))

    def own_copy(i):
        return pltpu.make_async_copy(a_ref.at[0, :, i], own.at[i], lsem.at[2 + i])

    w_copy = pltpu.make_async_copy(w_ref, wide, lsem.at[0])
    s_copy = pltpu.make_async_copy(s_ref.at[0], sens.at[pl.ds(2, cx)], lsem.at[1])
    w_copy.start()
    s_copy.start()
    for j in range(cx):
        own_copy(j).start()

    def plane_copy(source, slot, sem, device):
        return pltpu.make_async_remote_copy(
            src_ref=a_ref.at[0, :, source],
            dst_ref=planes.at[slot],
            send_sem=ssem.at[sem],
            recv_sem=rsem.at[slot],
            device_id=device,
            device_id_type=MESH,
        )

    def sens_copy(source, slot, sem, device):
        return pltpu.make_async_remote_copy(
            src_ref=s_ref.at[0, pl.ds(source, 2)],
            dst_ref=sens.at[pl.ds(slot, 2)],
            send_sem=ssem.at[total + sem],
            recv_sem=rsem.at[total + sem],
            device_id=device,
            device_id_type=MESH,
        )

    def to_high(j):
        return plane_copy(cx - STEPS + j, j, j, (before, high))

    def to_same(j):
        return plane_copy(j, STEPS + j, STEPS + j, (before, gx))

    def to_low(j):
        return plane_copy(j, STEPS + cx + j, STEPS + cx + j, (before, low))

    sens_to_high = sens_copy(cx - 2, 0, 0, (seg, high))
    sens_to_low = sens_copy(0, cx + 2, 1, (seg, low))

    pl.semaphore_wait(barrier, 1 + (2 + crosses.astype(jnp.int32)) * (lows + highs))

    @pl.when(has_high)
    def _():
        sens_to_high.start()

    @pl.when(has_low)
    def _():
        sens_to_low.start()

    for j in range(STEPS):

        @pl.when(has_high)
        def _():
            to_high(j).start()

        @pl.when(has_low)
        def _():
            to_low(j).start()

    for j in range(FIRST):
        to_same(j).start()

    @pl.when(jnp.logical_not(leaves))
    def _():
        for j in range(FIRST, cx):
            to_same(j).start()

    @pl.when(jnp.logical_not(has_low))
    def _():
        sens[pl.ds(0, 2)] = jnp.zeros((2, nt, nr), jnp.float32)
        planes[pl.ds(0, STEPS)] = jnp.zeros((STEPS, fields, nt, nr), jnp.float32)

    @pl.when(jnp.logical_not(has_high))
    def _():
        sens[pl.ds(cx + 2, 2)] = jnp.zeros((2, nt, nr), jnp.float32)
        planes[pl.ds(cx + STEPS, STEPS)] = jnp.zeros((STEPS, fields, nt, nr), jnp.float32)

    for step in range(STEPS):
        for slot in range(3 + STEPS):
            for f in range(fields):
                mixd[step, slot, f, pl.ds(0, 8)] = jnp.zeros((8, nr), jnp.float32)
                mixd[step, slot, f, pl.ds(8 + nt, 8)] = jnp.zeros((8, nr), jnp.float32)

    w_copy.wait()
    block = 64
    for i in range(nr // block):
        w = wide[pl.ds(i * block, block)]
        w_hi = w.astype(jnp.bfloat16)
        w_lo = (w - w_hi.astype(jnp.float32)).astype(jnp.bfloat16)
        wcat[pl.ds(i * block, block)] = w_hi
        wcat[pl.ds(nr + i * block, block)] = w_hi
        wcat[pl.ds(2 * nr + i * block, block)] = w_lo
    s_copy.wait()

    @pl.when(has_low)
    def _():
        sens_copy(cx - 2, 0, 0, (seg, high)).wait_recv()

    @pl.when(has_high)
    def _():
        sens_copy(0, cx + 2, 1, (seg, low)).wait_recv()

    def arrival(i):
        plane_copy(0, i, i, (before, gx)).wait_recv()

    def low_halo(first, stop, sem):
        @pl.when(has_low)
        def _():
            for j in range(first, stop):
                arrival(j)

        @pl.when(jnp.logical_and(leaves, has_low))
        def _():
            pl.semaphore_signal(gsem.at[sem], inc=1, device_id=(freed, low), device_id_type=MESH)

    def high_halo(first, stop, sem):
        @pl.when(has_high)
        def _():
            for j in range(first, stop):
                arrival(STEPS + cx + j)

        @pl.when(jnp.logical_and(leaves, has_high))
        def _():
            pl.semaphore_signal(gsem.at[sem], inc=1, device_id=(freed, high), device_id_type=MESH)

    def go(sem, count, start, stop):
        @pl.when(jnp.logical_and(leaves, count > 0))
        def _():
            pl.semaphore_wait(gsem.at[sem], count)

        @pl.when(leaves)
        def _():
            for j in range(start, stop):
                to_same(j).start()

    low_halo(0, STEPS - 1, 0)
    high_halo(0, STEPS - 1, 0)
    go(0, lows + highs, FIRST, FIRST + SECOND)
    low_halo(STEPS - 1, STEPS, 1)
    go(1, highs, FIRST + SECOND, cx)

    lane = lax.broadcasted_iota(jnp.int32, (half, nr), 1)

    def put(f, h, x):
        rows = pl.ds(f * nt + h * half, half)
        x_hi = x.astype(jnp.bfloat16)
        x_lo = (x - x_hi.astype(jnp.float32)).astype(jnp.bfloat16)
        xcat[rows, pl.ds(0, nr)] = x_hi
        xcat[rows, pl.ds(nr, nr)] = x_lo
        xcat[rows, pl.ds(2 * nr, nr)] = x_hi

    ahead = STEPS + cx

    def two_of(i):
        return jnp.where(i < ahead, lax.rem(i, 2), i - ahead + 2)

    def three_of(i):
        return jnp.where(i < ahead, lax.rem(i, 3), i - ahead + 3)

    def filter_and_mix(step, i):
        two, three = two_of(i), three_of(i)
        filt[step, two] = jnp.dot(xcat[...], wcat[...], preferred_element_type=jnp.float32).reshape(fields, nt, nr)
        for t in range(nt // 8):
            rows = pl.ds(t * 8, 8)
            v = [filt[step, two, g, rows] for g in range(fields)]
            for f in range(fields):
                m = c_ref[0, f] * v[0]
                for g in range(1, fields):
                    m = m + c_ref[g, f] * v[g]
                mixd[step, three, f, pl.ds(8 + t * 8, 8)] = m

    def stencil(step, i, use):
        two = two_of(i)
        mid, lo, hi = three_of(i), three_of(i - 1), three_of(i + 1)
        for h in range(2):
            s = sens[i - 1, pl.ds(h * half, half)]
            for f in range(fields):
                at = 8 + h * half
                m = mixd[step, mid, f, pl.ds(at, half)]
                total_ = mixd[step, lo, f, pl.ds(at, half)] + mixd[step, hi, f, pl.ds(at, half)]
                total_ = total_ + mixd[step, mid, f, pl.ds(at - 1, half)] + mixd[step, mid, f, pl.ds(at + 1, half)]
                left = jnp.where(lane == 0, 0.0, pltpu.roll(m, 1, 1))
                right = jnp.where(lane == nr - 1, 0.0, pltpu.roll(m, nr - 1, 1))
                total_ = total_ + left + right - 6.0 * m
                use(f, h, filt[step, two, f, pl.ds(h * half, half)] + s * total_)

    def first_step(i):
        for h in range(2):
            for f in range(fields):
                put(f, h, planes[i, f, pl.ds(h * half, half)])
        filter_and_mix(0, i)

    def early(i, carry):
        first_step(i)
        return carry

    lax.fori_loop(ahead, total - 1, early, 0)

    def last_halo():
        @pl.when(has_high)
        def _():
            arrival(total - 1)

        first_step(total - 1)
        stencil(0, total - 2, put)
        filter_and_mix(1, total - 2)

    pl.when(jnp.logical_not(leaves))(last_halo)

    def arrive(i, carry):
        @pl.when(i < ahead)
        def _():
            @pl.when(i >= STEPS)
            def _():
                arrival(i)

            first_step(i)

        @pl.when(jnp.logical_and(i >= 2, i < total - 1))
        def _():
            stencil(0, i - 1, put)
            filter_and_mix(1, i - 1)

        pl.when(jnp.logical_and(leaves, i == total - 1))(last_halo)

        @pl.when(i >= 4)
        def _():
            stencil(1, i - 2, put)
            filter_and_mix(2, i - 2)

        @pl.when(i >= 6)
        def _():
            o = i - 2 * STEPS
            pltpu.make_async_copy(a_ref.at[0, :, o], own.at[o], lsem.at[2 + o]).wait()

            def write(f, h, x):
                rows = pl.ds(h * half, half)
                out_ref[f, o, rows] = x - own[o, f, rows]

            stencil(2, i - 3, write)

        return carry

    lax.fori_loop(0, total, arrive, 0)

    @pl.when(has_high)
    def _():
        sens_to_high.wait_send()
        for j in range(STEPS):
            to_high(j).wait_send()

    for j in range(cx):
        to_same(j).wait_send()

    @pl.when(has_low)
    def _():
        sens_to_low.wait_send()
        for j in range(STEPS):
            to_low(j).wait_send()


def shards(adjoint_in, sensor, filter_matrix, coupling):
    _, fields, cx, nt, nr = adjoint_in.shape
    total = cx + 2 * STEPS
    out = pl.pallas_call(
        kernel,
        out_shape=pltpu.VMEM((fields, cx, nt, nr), jnp.float32),
        in_specs=[
            pl.BlockSpec(memory_space=pltpu.HBM),
            pl.BlockSpec(memory_space=pltpu.HBM),
            pl.BlockSpec(memory_space=pltpu.HBM),
            pl.BlockSpec(memory_space=pltpu.SMEM),
        ],
        out_specs=pl.BlockSpec(memory_space=pltpu.VMEM),
        scratch_shapes=[
            pltpu.VMEM((total, fields, nt, nr), jnp.float32),
            pltpu.VMEM((cx, fields, nt, nr), jnp.float32),
            pltpu.VMEM((cx + 4, nt, nr), jnp.float32),
            pltpu.VMEM((nr, nr), jnp.float32),
            pltpu.VMEM((3 * nr, nr), jnp.bfloat16),
            pltpu.VMEM((fields * nt, 3 * nr), jnp.bfloat16),
            pltpu.VMEM((STEPS, 2 + STEPS, fields, nt, nr), jnp.float32),
            pltpu.VMEM((STEPS, 3 + STEPS, fields, nt + 16, nr), jnp.float32),
            pltpu.SemaphoreType.DMA((total + 2,)),
            pltpu.SemaphoreType.DMA((total + 2,)),
            pltpu.SemaphoreType.DMA((cx + 2,)),
            pltpu.SemaphoreType.REGULAR((2,)),
        ],
        compiler_params=pltpu.CompilerParams(collective_id=0, has_side_effects=True, vmem_limit_bytes=61_400_000),
        name="shooting",
    )(adjoint_in, sensor, filter_matrix, coupling)
    return out[None]


def solution(mesh):
    in_specs = (P("seg", None, "gx", None, None), P("seg", "gx", None, None), P(), P())
    out_specs = P("seg", None, "gx", None, None)
    return jax.shard_map(shards, mesh=mesh, in_specs=in_specs, out_specs=out_specs, check_vma=False)
```
